32 devices in a mesh: dp: 32 (over z, y, x, core).
Axes of the slice: x: 2, y: 2, z: 4, core: 2. Of those that a mesh axis runs over, the one named last changes fastest.
Arguments:
- tokens: bfloat16 [16384, 768], P('dp'), may hold values from -6 to 6
- gain_attn: float32 [768], P('dp'), may hold values from 0.25 to 1.75
- w_query: float32 [768, 768], P('dp'), may hold values from -0.0390625 to 0.0390625
- w_key: float32 [768, 768], P('dp'), may hold values from -0.21875 to 0.21875
- w_value: float32 [768, 768], P('dp'), may hold values from -0.21875 to 0.21875
- w_out: float32 [768, 768], P('dp'), may hold values from -2.5 to 2.5
- bias_table: float32 [384], P('dp'), may hold values from -4 to 4
- gain_ffn: float32 [768], P('dp'), may hold values from 0.25 to 1.75
- w_gate: float32 [768, 2048], P('dp'), may hold values from -0.21875 to 0.21875
- w_up: float32 [768, 2048], P('dp'), may hold values from -0.21875 to 0.21875
- w_down: float32 [2048, 768], P('dp'), may hold values from -0.125 to 0.125
- cotangent: bfloat16 [16384, 768], P('dp'), may hold values from -6 to 6
- seq_lengths: int32 [8], replicated, may hold values from 1153 to 4096, as said below
- holders: int32 [8, 16], replicated, may hold values from 0 to 31, as said below
- offsets: int32 [8, 16], replicated, may hold values from 0 to 1
Outputs:
- output: bfloat16 [16384, 768], P('dp')
- grad_tokens: bfloat16 [16384, 768], P('dp')
- grad_gain_attn: float32 [768], P('dp')
- grad_query_w: float32 [768, 768], P('dp')
- grad_key_w: float32 [768, 768], P('dp')
- grad_value_w: float32 [768, 768], P('dp')
- grad_out_w: float32 [768, 768], P('dp')
- grad_table: float32 [384], P('dp')
- grad_gain_ffn: float32 [768], P('dp')
- grad_gate_w: float32 [768, 2048], P('dp')
- grad_up_w: float32 [768, 2048], P('dp')
- grad_down_w: float32 [2048, 768], P('dp')
The draws below stay inside these ranges and needn't reach their ends.
Inputs may be any that keep to these rules, and one draw needn't show every extreme that they name: Sequence s fills ceil(seq_lengths[s] / 256) whole blocks, from 5 to 16; the sequences lie one after another in the given order from block 0 and fill all 64 blocks; the last block of a sequence holds more than 128 of its rows; some sequence has 4096 tokens. holders[s, h] * 2 + offsets[s, h] is the given-order number of block h of sequence s; at and past the sequence's block count the entries repeat its last block.
All inputs are finite; a program needn't handle non-finite values.
Results may differ from the reference program's by a relative error of at most 0.015.
The reference program's roundings to bfloat16 on the way count: a program that leaves them out, or rounds other values in their place, can miss the bound.
Values may be sent and summed in bfloat16 or wider, within the bound.
A program may use at most 256 MiB of HBM per device.

```python
import jax
import jax.numpy as jnp
from jax import lax

D = 768
HEADS = 12
HEAD = 64
FF = 2048
BUCKETS = 32
BLOCK = 256
BLK_DEV = 2
HOLD = 16
MINB = 5
SPAN = 8
TOKENS = 16384
BLOCKS = 64
SEQS = 8


def layout(key):
    base_key = jax.random.fold_in(key, 1234)
    keys_list = jax.random.split(base_key, 5)
    group_count = SEQS // 4
    cap_extra = HOLD - MINB
    group_extra = 4 * (SPAN - MINB)
    first_extra = jax.random.randint(keys_list[0], (group_count,), max(group_extra - 3 * cap_extra, 0), cap_extra + 1)
    first_extra = first_extra.at[0].set(cap_extra)
    rest_one = group_extra - first_extra
    second_extra = jax.random.randint(keys_list[1], (group_count,), jnp.maximum(rest_one - 2 * cap_extra, 0), jnp.minimum(rest_one, cap_extra) + 1)
    rest_two = rest_one - second_extra
    third_extra = jax.random.randint(keys_list[2], (group_count,), jnp.maximum(rest_two - cap_extra, 0), jnp.minimum(rest_two, cap_extra) + 1)
    fourth_extra = rest_two - third_extra
    extras = jnp.stack([first_extra, second_extra, third_extra, fourth_extra], axis=1).reshape(SEQS)
    seq_order = jax.random.permutation(keys_list[3], SEQS)
    counts = (MINB + extras[seq_order]).astype(jnp.int32)
    tail_trims = jax.random.randint(keys_list[4], (SEQS,), 0, BLOCK // 2)
    tail_trims = jnp.where(seq_order == 0, 0, tail_trims)
    lengths = (counts * BLOCK - tail_trims).astype(jnp.int32)
    starts = jnp.cumsum(counts) - counts
    slot_index = jnp.minimum(jnp.arange(HOLD, dtype=jnp.int32)[None, :], counts[:, None] - 1)
    held_blocks = starts[:, None] + slot_index
    holder_ids = (held_blocks // BLK_DEV).astype(jnp.int32)
    slot_offsets = (held_blocks % BLK_DEV).astype(jnp.int32)
    return (lengths, holder_ids, slot_offsets)


def draw_seq_lengths(key, part):
    return layout(key)[0]


def draw_holders(key, part):
    return layout(key)[1]


def draw_offsets(key, part):
    return layout(key)[2]


def raised(values, rng, source, target, shards_of, factor):
    owner, partner = [(jnp.arange(values.shape[axis_at]) // (values.shape[axis_at] // shards_of)).reshape([-1 if axis == axis_at else 1 for axis in range(values.ndim)]) for axis_at in (source, target)]
    chosen = jax.random.permutation(rng, shards_of)[partner]
    strong = (owner == chosen) | (owner == (partner + shards_of // 2) % shards_of)
    return jnp.where(strong, factor * values, values)


def block_levels(stream_key, shape, cuts, smallest, largest):
    factor_of, own = 1.0, jax.random.fold_in(stream_key, 6)
    for dim, parts in cuts:
        heights = jnp.exp(jax.random.uniform(jax.random.fold_in(own, dim), (parts,), jnp.float32, smallest / len(cuts), largest / len(cuts)))
        factor_of = factor_of * jnp.repeat(heights, shape[dim] // parts).reshape([-1 if axis == dim else 1 for axis in range(len(shape))])
    return factor_of


def noise(stream_key, extent, deviation, bound, cuts=(), held_as=jnp.bfloat16):
    values = deviation * jax.random.normal(stream_key, extent, jnp.float32)
    if cuts:
        values = values * block_levels(stream_key, extent, cuts, -0.22, 0.18)
    return jnp.clip(values, -bound, bound).astype(held_as)


def noise_with(own_key, extent, width, limit, pieces, heavy, kind=jnp.bfloat16):
    result = width * jax.random.normal(own_key, extent, jnp.float32)
    if pieces:
        result = result * block_levels(own_key, extent, pieces, -0.22, 0.18)
    return jnp.clip(raised(result, jax.random.fold_in(own_key, 3), *heavy), -limit, limit).astype(kind)


def setup_inputs(seed: int = 0) -> dict:
    seeds = jax.random.split(jax.random.key(seed), 16)
    tokens = noise_with(seeds[0], (TOKENS, D), 1.0, 6.0, ((0, 32),), (0, 1, 32, 2.75))
    gain_attn = jnp.clip(1.0 + 0.15 * jax.random.normal(seeds[1], (D,), jnp.float32), 0.25, 1.75)
    w_query = noise(seeds[2], (D, D), (D * HEAD // 2) ** -0.5, 0.0390625, ((0, 32),), jnp.float32)
    w_key = noise(seeds[3], (D, D), D ** -0.5, 0.21875, ((0, 32),), jnp.float32)
    w_value = noise(seeds[4], (D, D), D ** -0.5, 0.21875, ((0, 32),), jnp.float32)
    w_out = noise(seeds[5], (D, D), (max(D // 128, 1)) ** -0.5, 2.5, ((0, 32),), jnp.float32)
    bias_table = noise(seeds[6], (BUCKETS * HEADS,), 1.0, 4.0, ((0, 32),), jnp.float32)
    gain_ffn = jnp.clip(1.0 + 0.15 * jax.random.normal(seeds[7], (D,), jnp.float32), 0.25, 1.75)
    w_gate = noise(seeds[8], (D, FF), D ** -0.5, 0.21875, ((0, 32),), jnp.float32)
    w_up = noise(seeds[9], (D, FF), D ** -0.5, 0.21875, ((0, 32),), jnp.float32)
    w_down = noise(seeds[10], (FF, D), FF ** -0.5, 0.125, ((0, 32),), jnp.float32)
    cotangent = noise(seeds[11], (TOKENS, D), 1.0, 6.0, ((0, 32),))
    seq_lengths = draw_seq_lengths(jax.random.fold_in(seeds[15], 71), 0)
    holders = draw_holders(jax.random.fold_in(seeds[15], 71), 0)
    offsets = draw_offsets(jax.random.fold_in(seeds[15], 71), 0)
    return {"tokens": tokens, "gain_attn": gain_attn, "w_query": w_query, "w_key": w_key, "w_value": w_value, "w_out": w_out, "bias_table": bias_table, "gain_ffn": gain_ffn, "w_gate": w_gate, "w_up": w_up, "w_down": w_down, "cotangent": cotangent, "seq_lengths": seq_lengths, "holders": holders, "offsets": offsets}


epsilon = 1e-06
MASKED = -1e+30
HIGHEST = lax.Precision.HIGHEST
far_steps = (12, 16, 23, 32, 46, 64, 91)

@jax.custom_vjp
def low(v):
    return lax.optimization_barrier(v.astype(jnp.bfloat16)).astype(jnp.float32)

@jax.custom_vjp
def low_back(v):
    return v

def low_keep(v):
    return (low(v), None)

def low_pass(kept, grad):
    return (grad,)

def back_keep(v):
    return (v, None)

def back_low(kept, grad):
    return (low(grad),)
low.defvjp(low_keep, low_pass)
low_back.defvjp(back_keep, back_low)

def bucket_of(relative):
    distance = jnp.abs(relative)
    far_bucket = jnp.full(relative.shape, 8, jnp.int32)
    for threshold in far_steps:
        far_bucket = far_bucket + (distance >= threshold).astype(jnp.int32)
    near_bucket = jnp.where(distance < 8, distance, far_bucket).astype(jnp.int32)
    return near_bucket + jnp.where(relative > 0, 16, 0).astype(jnp.int32)

def skew_bias(vector, row_count):
    lead_dim, span_all = vector.shape
    tiled_rows = jnp.broadcast_to(vector[:, None, :], (lead_dim, row_count, span_all))
    flat_rows = tiled_rows.reshape(lead_dim, row_count * span_all)[:, :row_count * (span_all - 1)]
    folded = flat_rows.reshape(lead_dim, row_count, span_all - 1)
    return folded[:, :, row_count - 1:span_all - 1]

def rms_norm(values, gain_vec):
    return values * lax.rsqrt(lax.optimization_barrier(jnp.mean(values * values, axis=-1, keepdims=True)) + epsilon) * gain_vec

def block_layer(token_vals, gain_attn, w_query, w_key, w_value, w_out, bias_table, gain_ffn, w_gate, w_up, w_down, seq_lengths, holders, offsets):
    attn_gain = low(gain_attn)
    query_proj = low(w_query)
    key_proj = low(w_key)
    value_proj = low(w_value)
    out_proj = low(w_out)
    table_full = low(bias_table).reshape(BUCKETS, HEADS)
    ffn_gain = low(gain_ffn)
    gate_proj = low(w_gate)
    up_proj = low(w_up)
    down_proj = low(w_down)
    attn_norm = low(rms_norm(token_vals, attn_gain))
    query_rows = low_back(low(jnp.dot(attn_norm, query_proj, precision=HIGHEST)))
    key_rows = low_back(low(jnp.dot(attn_norm, key_proj, precision=HIGHEST)))
    value_rows = low_back(low(jnp.dot(attn_norm, value_proj, precision=HIGHEST)))
    key_blocks = key_rows.reshape(BLOCKS, BLOCK, D)
    value_blocks = value_rows.reshape(BLOCKS, BLOCK, D)
    block_counts = ((seq_lengths + BLOCK - 1) // BLOCK).astype(jnp.int32)
    held_blocks = (holders * BLK_DEV + offsets).astype(jnp.int32)
    slot_ids = jnp.arange(HOLD, dtype=jnp.int32)[None, :]
    seq_ids = jnp.arange(SEQS, dtype=jnp.int32)[:, None]
    slot_live = slot_ids < block_counts[:, None]
    key_pos = jnp.arange(HOLD * BLOCK, dtype=jnp.int32)
    bias_pos = jnp.arange(HOLD * BLOCK + BLOCK, dtype=jnp.int32)

    def one_block(block_id):
        matches = (held_blocks == block_id) & slot_live
        owner_seq = jnp.sum(jnp.where(matches, seq_ids, 0)).astype(jnp.int32)
        block_place = jnp.sum(jnp.where(matches, slot_ids, 0)).astype(jnp.int32)
        fetch_rows = held_blocks[owner_seq]
        key_block = low_back(key_blocks[fetch_rows]).reshape(HOLD * BLOCK, HEADS, HEAD)
        value_block = low_back(value_blocks[fetch_rows]).reshape(HOLD * BLOCK, HEADS, HEAD)
        query_block = low_back(lax.dynamic_slice_in_dim(query_rows, (block_id * BLOCK).astype(jnp.int32), BLOCK, 0)).reshape(BLOCK, HEADS, HEAD)
        bucket_ids = bucket_of((bias_pos - (BLOCK - 1) - block_place * BLOCK).astype(jnp.int32))
        bias_vec = jnp.transpose(table_full[bucket_ids])
        scores = jnp.einsum('qhd,khd->hqk', query_block, key_block, precision=HIGHEST) + skew_bias(bias_vec, BLOCK)
        scores = low_back(scores)
        valid_keys = key_pos < seq_lengths[owner_seq]
        scores = jnp.where(valid_keys[None, None, :], scores, MASKED)
        row_max = lax.optimization_barrier(jnp.max(scores, axis=-1, keepdims=True))
        exp_terms = jnp.exp(scores - row_max)
        soft_probs = exp_terms / lax.optimization_barrier(jnp.sum(exp_terms, axis=-1, keepdims=True))
        head_out = jnp.einsum('hqk,khd->qhd', low(soft_probs), value_block, precision=HIGHEST)
        return head_out.reshape(BLOCK, D)
    attended = lax.map(jax.checkpoint(one_block), jnp.arange(BLOCKS, dtype=jnp.int32))
    attended = low_back(low(attended.reshape(TOKENS, D)))
    hidden_one = token_vals + low_back(jnp.dot(attended, out_proj, precision=HIGHEST))
    ffn_norm = low(rms_norm(hidden_one, ffn_gain))
    gate_val = low_back(jnp.dot(ffn_norm, gate_proj, precision=HIGHEST))
    up_val = low_back(jnp.dot(ffn_norm, up_proj, precision=HIGHEST))
    inner_act = low(jax.nn.gelu(gate_val, approximate=True) * up_val)
    return hidden_one + low_back(jnp.dot(inner_act, down_proj, precision=HIGHEST))

def reference(tokens, gain_attn, w_query, w_key, w_value, w_out, bias_table, gain_ffn, w_gate, w_up, w_down, cotangent, seq_lengths, holders, offsets):

    def forward(token_vals, gain_one, query_m, key_m, value_m, out_m, table_m, gain_two, gate_m, up_m, down_m):
        return block_layer(token_vals, gain_one, query_m, key_m, value_m, out_m, table_m, gain_two, gate_m, up_m, down_m, seq_lengths, holders, offsets)
    output, pullback = jax.vjp(forward, tokens.astype(jnp.float32), gain_attn, w_query, w_key, w_value, w_out, bias_table, gain_ffn, w_gate, w_up, w_down)
    grads = pullback(cotangent.astype(jnp.float32))
    return (output.astype(jnp.bfloat16), grads[0].astype(jnp.bfloat16), grads[1], grads[2], grads[3], grads[4], grads[5], grads[6], grads[7], grads[8], grads[9], grads[10])
```

```python
import functools

import jax
import jax.numpy as jnp
from jax import lax
from jax.experimental import pallas as pl
from jax.experimental.pallas import tpu as pltpu
from jax.sharding import PartitionSpec as P

HEADS = 12
HEAD = 64
BUCKETS = 32
BLOCK = 256
BLK_DEV = 2
HOLD = 16
LANES = 128

GROUP = HOLD // BLK_DEV
CHIPS = GROUP // 2
PER_CHIP = HEADS // CHIPS
HALF = HOLD // 2
ITEMS = HOLD + HALF

epsilon = 1e-06
MASKED = -1e30
far_steps = (12, 16, 23, 32, 46, 64, 91)
BEGINS = tuple(range(9)) + far_steps
BF = jnp.bfloat16
F32 = jnp.float32


def full_head(p):
    return PER_CHIP * (p // 2) + 2 * (p % 2)


def shared_head(p):
    return PER_CHIP * (p // 2) + 1


HEAD_ORDER = [h for p in range(GROUP) for h in (full_head(p), shared_head(p))]


def norm_apply(values, gain_vec):
    return (
        values * lax.rsqrt(jnp.mean(values * values, axis=-1, keepdims=True) + epsilon) * gain_vec
    )


def gated_linear_unit(gate_val, up_val):
    return jax.nn.gelu(gate_val, approximate=True) * up_val


def fill_layout(len_ref, zone, meta):
    seqs = len_ref.shape[0]
    base = zone * HOLD
    for i in range(HOLD):
        block = base + i

        def look(s, carry):
            start, first, count, rest = carry
            length = len_ref[s]
            blocks = (length + BLOCK - 1) // BLOCK
            inside = jnp.logical_and(block >= start, block < start + blocks)
            first = jnp.where(inside, start - base + HOLD, first)
            count = jnp.where(inside, blocks, count)
            rest = jnp.where(inside, length - (blocks - 1) * BLOCK, rest)
            return (start + blocks, first, count, rest)

        zero = jnp.int32(0)
        _, first, count, rest = lax.fori_loop(0, seqs, look, (zero, zero, zero, zero))
        meta[0, i] = first
        meta[1, i] = count
        meta[2, i] = rest


def fill_bias(tab_ref, bias, keys_first):
    rows = lax.broadcasted_iota(jnp.int32, (BLOCK, BLOCK), 0)
    cols = lax.broadcasted_iota(jnp.int32, (BLOCK, BLOCK), 1)
    rel = rows - cols if keys_first else cols - rows
    for h in range(2):
        for t in range(5):
            if t == 0:
                tile = jnp.full((BLOCK, BLOCK), tab_ref[h, 15], F32)
            elif t == 4:
                tile = jnp.full((BLOCK, BLOCK), tab_ref[h, 31], F32)
            else:
                diff = rel + (t - 2) * BLOCK
                tile = jnp.full((BLOCK, BLOCK), tab_ref[h, 0], F32)
                if t <= 2:
                    for b in range(1, 16):
                        tile = jnp.where(diff <= -BEGINS[b], tab_ref[h, b], tile)
                if t >= 2:
                    for b in range(1, 16):
                        tile = jnp.where(diff >= BEGINS[b], tab_ref[h, 16 + b], tile)
            bias[h, t] = tile


def item_of(j, core):
    shared = j >= HOLD
    h = jnp.where(shared, 1, 0)
    i = jnp.where(shared, 2 * (j - HOLD) + core, j)
    return h, i


def relation(e, own):
    return jnp.clip(e - own, -2, 2) + 2


def head_lanes(h):
    lane = lax.broadcasted_iota(jnp.int32, (BLOCK, LANES), 1)
    return (lane >= HEAD) == (h == 1)


def last_bias(bias, h, rel, valid, keys_first):
    pos = lax.broadcasted_iota(jnp.int32, (BLOCK, BLOCK), 0 if keys_first else 1)
    bias[h, 5] = jnp.where(pos < valid, bias[h, rel], MASKED)


def window_copies(mid, low, high, window, sem):
    return [
        pltpu.make_async_copy(src, window.at[pl.ds(s * HOLD * BLOCK, HOLD * BLOCK)], sem.at[s])
        for s, src in ((1, mid), (0, low), (2, high))
    ]


def forward_kernel(
    len_ref, tab_ref, place_ref, q_ref, mid, low, high, o_ref, lse_ref,
    window, ones_v, bias, scores, meta, sem,
):
    copies = window_copies(mid, low, high, window, sem)
    for copy in copies:
        copy.start()
    core = place_ref[1]
    fill_layout(len_ref, place_ref[0], meta)
    fill_bias(tab_ref, bias, False)
    for copy in copies:
        copy.wait()
    lane = lax.broadcasted_iota(jnp.int32, (BLOCK, LANES), 1)

    def split(e, _):
        rows = pl.ds(pl.multiple_of(e * BLOCK, BLOCK), BLOCK)
        v = window[rows, LANES:]
        ones_v[0, rows] = jnp.where(lane < HEAD, v, jnp.ones_like(v))
        ones_v[1, rows] = jnp.where(lane < HEAD, jnp.ones_like(v), v)
        return 0

    lax.fori_loop(0, 3 * HOLD, split, 0)

    def item(j, _):
        h, i = item_of(j, core)
        rows = pl.ds(pl.multiple_of(i * BLOCK, BLOCK), BLOCK)
        first, count, valid = meta[0, i], meta[1, i], meta[2, i]
        own = HOLD + i
        mine = head_lanes(h)
        q = q_ref[rows]
        q = jnp.where(mine, q, jnp.zeros_like(q))
        last_bias(bias, h, relation(first + count - 1, own), valid, False)

        def score(t, peak):
            e = first + t
            k = window[pl.ds(pl.multiple_of(e * BLOCK, BLOCK), BLOCK), :LANES]
            s = lax.dot_general(q, k, (((1,), (1,)), ((), ())), preferred_element_type=F32)
            s = s + bias[h, jnp.where(t == count - 1, 5, relation(e, own))]
            scores[t] = s
            return jnp.maximum(peak, jnp.maximum(s[:, :LANES], s[:, LANES:]))

        peak = lax.fori_loop(0, count, score, jnp.full((BLOCK, LANES), -3e38, F32))
        top = jnp.broadcast_to(jnp.max(peak, axis=1, keepdims=True), (BLOCK, LANES))

        def mix(t, acc):
            e = first + t
            s = scores[t]
            p = jnp.concatenate([jnp.exp(s[:, :LANES] - top), jnp.exp(s[:, LANES:] - top)], axis=1)
            v = ones_v[h, pl.ds(pl.multiple_of(e * BLOCK, BLOCK), BLOCK)]
            return acc + jnp.dot(p.astype(BF), v, preferred_element_type=F32)

        acc = lax.fori_loop(0, count, mix, jnp.zeros((BLOCK, LANES), F32))
        total = jnp.where(mine, pltpu.roll(acc, HEAD, 1), acc)
        out = jnp.where(mine, acc / total, 0.0)
        lse = jnp.transpose(top + jnp.log(total))
        lse_ref[j] = lse[:8]

        @pl.when(h == 0)
        def _():
            o_ref[rows] = out

        @pl.when(h == 1)
        def _():
            o_ref[rows] = o_ref[rows] + out

        return 0

    lax.fori_loop(0, ITEMS, item, 0)


def backward_kernel(
    len_ref, tab_ref, place_ref, q_ref, g_ref, o_ref, lse_ref, mid, low, high,
    dq_ref, dmid, dlow, dhigh, dtab_ref,
    window, flipped, bias, grads, sums, out_mid, out_far, meta, sem, out_sem,
):
    copies = window_copies(mid, low, high, window, sem)
    for copy in copies:
        copy.start()
    core = place_ref[1]
    fill_layout(len_ref, place_ref[0], meta)
    fill_bias(tab_ref, bias, True)
    sums[...] = jnp.zeros_like(sums)
    for copy in copies:
        copy.wait()

    def flip(e, _):
        at = pl.multiple_of(e * BLOCK, BLOCK)
        flipped[:, pl.ds(at, BLOCK)] = jnp.transpose(window[pl.ds(at, BLOCK), :LANES])
        grads[pl.ds(at, BLOCK)] = jnp.zeros((BLOCK, 2 * LANES), F32)
        return 0

    lax.fori_loop(0, 3 * HOLD, flip, 0)

    def item(j, _):
        h, i = item_of(j, core)
        rows = pl.ds(pl.multiple_of(i * BLOCK, BLOCK), BLOCK)
        first, count, valid = meta[0, i], meta[1, i], meta[2, i]
        own = HOLD + i
        mine = head_lanes(h)
        q = q_ref[rows]
        q = jnp.where(mine, q, jnp.zeros_like(q))
        g = g_ref[rows]
        g = jnp.where(mine, g, jnp.zeros_like(g))
        last_bias(bias, h, relation(first + count - 1, own), valid, True)
        lse = lse_ref[j][:1]
        delta = jnp.sum(jnp.transpose(g.astype(F32) * o_ref[rows]), axis=0, keepdims=True)

        def step(t, dq):
            e = first + t
            at = pl.ds(pl.multiple_of(e * BLOCK, BLOCK), BLOCK)
            rel = relation(e, own)
            k = window[at, :LANES]
            v = window[at, LANES:]
            s = lax.dot_general(k, q, (((1,), (1,)), ((), ())), preferred_element_type=F32)
            s = s + bias[h, jnp.where(t == count - 1, 5, rel)]
            p = jnp.exp(s - lse)
            dp = lax.dot_general(v, g, (((1,), (1,)), ((), ())), preferred_element_type=F32)
            ds = p * (dp - delta)
            sums[h, rel] = sums[h, rel] + ds
            ds = ds.astype(BF)
            grads[at, LANES:] = grads[at, LANES:] + jnp.dot(
                p.astype(BF), g, preferred_element_type=F32
            )
            grads[at, :LANES] = grads[at, :LANES] + jnp.dot(ds, q, preferred_element_type=F32)
            return dq + jnp.dot(flipped[:, at], ds, preferred_element_type=F32)

        dq = lax.fori_loop(0, count, step, jnp.zeros((LANES, BLOCK), F32))
        dq = jnp.where(mine, jnp.transpose(dq), 0.0).astype(BF)

        @pl.when(h == 0)
        def _():
            dq_ref[rows] = dq

        @pl.when(h == 1)
        def _():
            dq_ref[rows] = dq_ref[rows] + dq

        return 0

    lax.fori_loop(0, ITEMS, item, 0)

    size = HOLD * BLOCK
    out_mid[...] = grads[pl.ds(size, size)]
    out_far[0] = grads[pl.ds(0, size)].astype(BF)
    out_far[1] = grads[pl.ds(2 * size, size)].astype(BF)
    outs = [
        pltpu.make_async_copy(out_mid, dmid, out_sem.at[0]),
        pltpu.make_async_copy(out_far.at[0], dlow, out_sem.at[1]),
        pltpu.make_async_copy(out_far.at[1], dhigh, out_sem.at[2]),
    ]
    for copy in outs:
        copy.start()

    rel = lax.broadcasted_iota(jnp.int32, (BLOCK, BLOCK), 0) - lax.broadcasted_iota(
        jnp.int32, (BLOCK, BLOCK), 1
    )
    spot = lax.broadcasted_iota(jnp.int32, (8, LANES), 0) * LANES + lax.broadcasted_iota(
        jnp.int32, (8, LANES), 1
    )
    found = jnp.zeros((8, LANES), F32)

    def fold(x):
        part = x[:8]
        for r in range(1, BLOCK // 8):
            part = part + x[r * 8 : r * 8 + 8]
        return part[:, :LANES] + part[:, LANES:]

    for h in range(2):
        for b in range(BUCKETS):
            if b == BUCKETS // 2:
                continue
            near = b % 16
            after = b >= 16
            part = jnp.zeros((8, LANES), F32)
            for t in (2, 3 if after else 1):
                diff = rel + (t - 2) * BLOCK
                far = diff if after else -diff
                if t != 2 and near == 0:
                    continue
                if near < 15:
                    inside = jnp.logical_and(far >= BEGINS[near], far < BEGINS[near + 1])
                else:
                    inside = far >= BEGINS[near]
                part = part + fold(jnp.where(inside, sums[h, t], 0.0))
            if near == 15:
                part = part + fold(sums[h, 4 if after else 0])
            found = jnp.where(spot == h * BUCKETS + b, jnp.sum(part), found)
    dtab_ref[...] = found
    for copy in outs:
        copy.wait()


ANY = pl.BlockSpec(memory_space=pl.ANY)
VMEM = pl.BlockSpec(memory_space=pltpu.VMEM)
SMEM = pl.BlockSpec(memory_space=pltpu.SMEM)
ROWS = HOLD * BLOCK


def forward_attention(lengths, table, place, q, mid, low, high):
    return pl.pallas_call(
        forward_kernel,
        out_shape=(
            jax.ShapeDtypeStruct((ROWS, LANES), F32),
            jax.ShapeDtypeStruct((ITEMS, 8, BLOCK), F32),
        ),
        in_specs=[SMEM, SMEM, SMEM, VMEM, ANY, ANY, ANY],
        out_specs=(VMEM, VMEM),
        scratch_shapes=[
            pltpu.VMEM((3 * ROWS, 2 * LANES), BF),
            pltpu.VMEM((2, 3 * ROWS, LANES), BF),
            pltpu.VMEM((2, 6, BLOCK, BLOCK), F32),
            pltpu.VMEM((HOLD, BLOCK, BLOCK), F32),
            pltpu.SMEM((3, HOLD), jnp.int32),
            pltpu.SemaphoreType.DMA((3,)),
        ],
        compiler_params=pltpu.CompilerParams(vmem_limit_bytes=56 << 20),
        name="forward_attention",
    )(lengths, table, place, q, mid, low, high)


def backward_attention(lengths, table, place, q, g, o, lse, mid, low, high):
    return pl.pallas_call(
        backward_kernel,
        out_shape=(
            jax.ShapeDtypeStruct((ROWS, LANES), BF),
            jax.ShapeDtypeStruct((ROWS, 2 * LANES), F32),
            jax.ShapeDtypeStruct((ROWS, 2 * LANES), BF),
            jax.ShapeDtypeStruct((ROWS, 2 * LANES), BF),
            jax.ShapeDtypeStruct((8, LANES), F32),
        ),
        in_specs=[SMEM, SMEM, SMEM, VMEM, VMEM, VMEM, VMEM, ANY, ANY, ANY],
        out_specs=(VMEM, ANY, ANY, ANY, VMEM),
        scratch_shapes=[
            pltpu.VMEM((3 * ROWS, 2 * LANES), BF),
            pltpu.VMEM((LANES, 3 * ROWS), BF),
            pltpu.VMEM((2, 6, BLOCK, BLOCK), F32),
            pltpu.VMEM((3 * ROWS, 2 * LANES), F32),
            pltpu.VMEM((2, 5, BLOCK, BLOCK), F32),
            pltpu.VMEM((ROWS, 2 * LANES), F32),
            pltpu.VMEM((2, ROWS, 2 * LANES), BF),
            pltpu.SMEM((3, HOLD), jnp.int32),
            pltpu.SemaphoreType.DMA((3,)),
            pltpu.SemaphoreType.DMA((3,)),
        ],
        compiler_params=pltpu.CompilerParams(vmem_limit_bytes=60 << 20),
        name="backward_attention",
    )(lengths, table, place, q, g, o, lse, mid, low, high)


def spread_heads(matrix):
    return jnp.concatenate([matrix[:, h * HEAD : (h + 1) * HEAD] for h in HEAD_ORDER], axis=1)


def join_heads(matrix):
    pieces = {}
    for at, h in enumerate(HEAD_ORDER):
        piece = matrix[:, at * HEAD : (at + 1) * HEAD]
        pieces[h] = pieces[h] + piece if h in pieces else piece
    return jnp.concatenate([pieces[h] for h in range(HEADS)], axis=1)


def shards(
    tokens, gain_attn, w_query, w_key, w_value, w_out, bias_table, gain_ffn,
    w_gate, w_up, w_down, cotangent, seq_lengths, holders, offsets,
):
    devices = lax.axis_size("dp")
    me = lax.axis_index("dp")
    rows_dev, width = tokens.shape
    zones = devices // GROUP
    groups = [list(range(z * GROUP, (z + 1) * GROUP)) for z in range(zones)]
    upward = [(d, d + GROUP) for d in range(devices - GROUP)]
    downward = [(d + GROUP, d) for d in range(devices - GROUP)]
    zone = me // GROUP
    member = me % GROUP
    place = jnp.stack([zone, member % 2]).astype(jnp.int32)
    lane_rows = GROUP * LANES
    part = width // devices
    ff = w_gate.shape[1]

    half = lambda a: a.astype(BF)
    small = jnp.concatenate(
        [
            half(gain_attn)[:, None],
            half(gain_ffn)[:, None],
            jnp.pad(half(bias_table), (0, part - bias_table.shape[0]))[:, None],
            jnp.zeros((part, LANES - 3), BF),
        ],
        axis=1,
    )
    first = jnp.concatenate(
        [spread_heads(half(w_query)), spread_heads(half(w_key)), spread_heads(half(w_value)), small],
        axis=1,
    )
    first = lax.all_gather(first, "dp", axis=0, tiled=True)
    second = jnp.concatenate([half(w_out), half(w_gate), half(w_up)], axis=1)
    second = lax.all_gather(second, "dp", axis=0, tiled=True)
    down = lax.all_gather(half(w_down), "dp", axis=0, tiled=True)

    w_q, w_k, w_v = (first[:, n * lane_rows : (n + 1) * lane_rows] for n in range(3))
    extra = first[:, 3 * lane_rows :]
    attn_gain = extra[:, 0].astype(F32)
    ffn_gain = extra[:, 1].astype(F32)
    table = extra[:, 2].reshape(devices, part)[:, : bias_table.shape[0]].reshape(BUCKETS, HEADS)
    table = table.astype(F32)
    chip = member // 2
    mine = jnp.stack([PER_CHIP * chip + 2 * (member % 2), PER_CHIP * chip + 1])
    my_table = jnp.transpose(jnp.take(table, mine, axis=1))

    inputs = tokens.astype(F32)
    attn_norm = norm_apply(inputs, attn_gain).astype(BF)

    def by_member(w):
        return jnp.einsum(
            "rd,dpc->prc", attn_norm, w.reshape(width, GROUP, -1), preferred_element_type=F32
        ).astype(BF)

    swap = functools.partial(
        lax.all_to_all, axis_name="dp", split_axis=0, concat_axis=0,
        axis_index_groups=groups, tiled=True,
    )
    q8 = by_member(w_q)
    kv8 = jnp.concatenate([by_member(w_k), by_member(w_v)], axis=-1)
    q = swap(q8).reshape(ROWS, LANES)
    mid = swap(kv8).reshape(ROWS, 2 * LANES)
    low = lax.ppermute(mid, "dp", upward)
    high = lax.ppermute(mid, "dp", downward)
    out, lse = forward_attention(seq_lengths, my_table, place, q, mid, low, high)

    attended = swap(out.astype(BF).reshape(GROUP, rows_dev, LANES))
    attended = jnp.transpose(attended, (1, 0, 2)).reshape(rows_dev, lane_rows)
    w_o = second[:, :width]
    w_o8 = jnp.concatenate([w_o[h * HEAD : (h + 1) * HEAD] for h in HEAD_ORDER], axis=0)
    w_g = second[:, width : width + ff]
    w_u = second[:, width + ff :]
    hidden_one = inputs + jnp.dot(attended, w_o8, preferred_element_type=F32)
    ffn_norm = norm_apply(hidden_one, ffn_gain).astype(BF)
    gate_val = jnp.dot(ffn_norm, w_g, preferred_element_type=F32)
    up_val = jnp.dot(ffn_norm, w_u, preferred_element_type=F32)
    inner_act = gated_linear_unit(gate_val, up_val).astype(BF)
    result = (hidden_one + jnp.dot(inner_act, down, preferred_element_type=F32)).astype(BF)

    cot = cotangent
    grad_down_w = jnp.dot(inner_act.T, cot, preferred_element_type=F32)
    grad_inner = jnp.dot(cot, down.T, preferred_element_type=F32)
    grad_gate, grad_up = jax.vjp(gated_linear_unit, gate_val, up_val)[1](grad_inner)
    grad_gate = grad_gate.astype(BF)
    grad_up = grad_up.astype(BF)
    grad_gate_w = jnp.dot(ffn_norm.T, grad_gate, preferred_element_type=F32)
    grad_up_w = jnp.dot(ffn_norm.T, grad_up, preferred_element_type=F32)
    grad_ffn_norm = jnp.dot(grad_gate, w_g.T, preferred_element_type=F32) + jnp.dot(
        grad_up, w_u.T, preferred_element_type=F32
    )
    grad_part, grad_gain_ffn = jax.vjp(norm_apply, hidden_one, ffn_gain)[1](grad_ffn_norm)
    grad_hidden = cot.astype(F32) + grad_part
    grad_branch = grad_hidden.astype(BF)
    grad_out_w = jnp.dot(attended.T, grad_branch, preferred_element_type=F32)
    grad_out_w = join_heads(grad_out_w.T).T
    scatter = functools.partial(lax.psum_scatter, axis_name="dp", scatter_dimension=0, tiled=True)
    early = scatter(
        jnp.concatenate([half(grad_out_w), half(grad_gate_w), half(grad_up_w)], axis=1)
    )
    late_down = scatter(half(grad_down_w))

    g8 = jnp.einsum(
        "rd,pcd->prc", grad_branch, w_o8.reshape(GROUP, LANES, width), preferred_element_type=F32
    ).astype(BF)
    g = swap(g8).reshape(ROWS, LANES)
    dq, dmid, dlow, dhigh, dtab = backward_attention(
        seq_lengths, my_table, place, q, g, out, lse, mid, low, high
    )
    dmid = dmid + lax.ppermute(dlow, "dp", downward).astype(F32)
    dmid = dmid + lax.ppermute(dhigh, "dp", upward).astype(F32)
    dqkv = jnp.concatenate([dq, dmid.astype(BF)], axis=1).reshape(GROUP, rows_dev, 3 * LANES)
    dqkv = jnp.transpose(swap(dqkv), (1, 0, 2))
    dq8, dk8, dv8 = (
        dqkv[:, :, n * LANES : (n + 1) * LANES].reshape(rows_dev, lane_rows) for n in range(3)
    )
    grad_q_w = join_heads(jnp.dot(attn_norm.T, dq8, preferred_element_type=F32))
    grad_k_w = join_heads(jnp.dot(attn_norm.T, dk8, preferred_element_type=F32))
    grad_v_w = join_heads(jnp.dot(attn_norm.T, dv8, preferred_element_type=F32))
    grad_attn_norm = (
        jnp.dot(dq8, w_q.T, preferred_element_type=F32)
        + jnp.dot(dk8, w_k.T, preferred_element_type=F32)
        + jnp.dot(dv8, w_v.T, preferred_element_type=F32)
    )
    grad_inputs, grad_gain_attn = jax.vjp(norm_apply, inputs, attn_gain)[1](grad_attn_norm)
    grad_tokens = (grad_hidden + grad_inputs).astype(BF)

    dtab = dtab.reshape(-1)[: 2 * BUCKETS].reshape(2, BUCKETS)
    one = (mine[:, None] == jnp.arange(HEADS)[None, :]).astype(F32)
    table_all = jnp.sum(dtab[:, :, None] * one[:, None, :], axis=0).reshape(devices, -1)
    table_all = jnp.pad(table_all, ((0, 0), (0, part - table_all.shape[1]))).reshape(-1)
    tiny = jnp.stack([grad_gain_attn, grad_gain_ffn, table_all], axis=1)
    top = half(tiny)
    tiny = jnp.concatenate(
        [top, half(tiny - top.astype(F32)), jnp.zeros((width, LANES - 6), BF)], axis=1
    )
    late = scatter(
        jnp.concatenate([half(grad_q_w), half(grad_k_w), half(grad_v_w), tiny], axis=1)
    ).astype(F32)
    early = early.astype(F32)
    tail = late[:, 3 * width :]
    tail = tail[:, :3] + tail[:, 3:6]
    return (
        result,
        grad_tokens,
        tail[:, 0],
        late[:, :width],
        late[:, width : 2 * width],
        late[:, 2 * width : 3 * width],
        early[:, :width],
        tail[: bias_table.shape[0], 2],
        tail[:, 1],
        early[:, width : width + ff],
        early[:, width + ff :],
        late_down.astype(F32),
    )


def solution(mesh):
    split = P("dp", None)
    line = P("dp")
    return jax.shard_map(
        shards,
        mesh=mesh,
        in_specs=(
            split, line, split, split, split, split, line, line,
            split, split, split, split, P(), P(), P(),
        ),
        out_specs=(
            split, split, line, split, split, split, split, line, line, split, split, split,
        ),
        check_vma=False,
    )
```
